32 devices in a mesh: parts: 2 (over x), node: 4 (over z), local: 4 (over y, core).
Axes of the slice: x: 2, y: 2, z: 4, core: 2. Of those that a mesh axis runs over, the one named last changes fastest.
Arguments:
- tokens: bfloat16 [256, 7168], P(('parts', 'node', 'local')), parts along dimension 0, may hold values from -6 to 6
- expert_ids: int32 [256, 8], P(('parts', 'node', 'local')), parts along dimension 0, may hold values from 0 to 7, as said below
- gate_weights: bfloat16 [256, 8], P(('parts', 'node', 'local')), parts along dimension 0, may hold values from 0.099609375 to 1
- slots: int32 [256, 4], P(('parts', 'node', 'local')), parts along dimension 0, may hold values from 0 to 8, as said below
- w_gate: bfloat16 [16, 7168, 2048], P(('parts', 'node'), None, 'local'), parts along dimension 0, may hold values from -0.0625 to 0.0625
- w_up: bfloat16 [16, 7168, 2048], P(('parts', 'node'), None, 'local'), parts along dimension 0, may hold values from -0.0625 to 0.0625
- w_down: bfloat16 [16, 2048, 7168], P(('parts', 'node'), 'local'), parts along dimension 0, may hold values from -0.125 to 0.125
Outputs:
- combined: bfloat16 [256, 7168], P(('parts', 'node', 'local')), parts along dimension 0
The draws below stay inside these ranges and needn't reach their ends.
There are 2 independent parts, one for each index of `parts`. The reference program is written for one: setup_inputs(seed, part) draws one part's arguments, and reference() takes and returns one part's arrays. A program takes and returns all parts, laid end to end along the dimension named above; each array names one. Nothing has to cross between parts.
Inputs may be any that keep to these rules, and one draw needn't show every extreme that they name: `expert_ids`: each row names 8 different experts, all within at most 4 node groups; expert e belongs to node group e // 2. slots[t, n] is below 8 exactly where some expert of token t belongs to node group n, and equals 8 elsewhere; within each aligned block of 8 rows (the rows of one device) the values below 8 in one column are distinct.
All inputs are finite; a program needn't handle non-finite values.
Results may differ from the reference program's by a relative error of at most 0.019.
Values may be sent and summed in bfloat16 or wider, within the bound.
A program may use at most 192 MiB of HBM per device.

```python
import math
import jax
import jax.numpy as jnp
from jax import lax

D = 7168
FF = 2048
EXP_NODE = 2
TOP = 8
GROUPS = 4
TOK_DEV = 8
TOKENS = 128
EXPERTS = 8
N_NODE = 4
N_LOCAL = 4


def routing(key):
    base_key = jax.random.fold_in(key, 7)
    row_keys = jax.random.split(base_key, TOKENS)

    def one_row(row_key):
        first_key, second_key = jax.random.split(row_key)
        chosen_groups = jax.random.permutation(first_key, N_NODE)[:GROUPS]
        picked = jax.random.permutation(second_key, GROUPS * EXP_NODE)[:TOP]
        candidates = (chosen_groups[:, None] * EXP_NODE + jnp.arange(EXP_NODE)[None, :]).reshape(-1)
        return candidates[picked]
    return jax.vmap(one_row)(row_keys).astype(jnp.int32)


def draw_expert_ids(key, part):
    return routing(key)


def draw_slots(key, part):
    chosen = routing(key)
    owners = chosen // EXP_NODE
    reach = jnp.any(owners[:, :, None] == jnp.arange(N_NODE)[None, None, :], axis=1).astype(jnp.int32)
    blocks = reach.reshape(TOKENS // TOK_DEV, TOK_DEV, N_NODE)
    order_key = jax.random.fold_in(key, 11)
    block_keys = jax.random.split(order_key, TOKENS // TOK_DEV * N_NODE)

    def one_order(order_seed):
        return jax.random.permutation(order_seed, TOK_DEV).astype(jnp.int32)
    priority = jax.vmap(one_order)(block_keys).reshape(TOKENS // TOK_DEV, N_NODE, TOK_DEV)
    priority = jnp.transpose(priority, (0, 2, 1))
    scores = priority + (1 - blocks) * TOK_DEV
    ordering = jnp.argsort(scores, axis=1, stable=True)
    ranked = jnp.argsort(ordering, axis=1, stable=True).astype(jnp.int32)
    placed = jnp.where(blocks > 0, ranked, TOK_DEV)
    return placed.reshape(TOKENS, N_NODE).astype(jnp.int32)


def steps_of(key, extent, cuts, least, top_value):
    gain = 1.0
    for position, parts in cuts:
        draws = jax.random.uniform(jax.random.fold_in(jax.random.fold_in(key, 6), position), (parts,), jnp.float32, least / len(cuts), top_value / len(cuts))
        gain = gain * jnp.repeat(jnp.exp(draws), extent[position] // parts).reshape((-1,) + (1,) * (len(extent) - 1 - position))
    return gain


def noise(key, dims, scale, limit, shards=(), held_as=jnp.bfloat16):
    drawn = scale * jax.random.normal(key, dims, jnp.float32)
    if shards:
        drawn = drawn * steps_of(key, dims, shards, -0.22, 0.18)
    return jnp.clip(drawn, -limit, limit).astype(held_as)


def setup_inputs(seed: int = 0, part: int = 0) -> dict:
    arg_keys = jax.random.split(jax.random.key(seed), 8)
    part_splits = jax.random.split(jax.random.fold_in(arg_keys[7], part), 8)
    return {
        "tokens": noise(part_splits[0], (TOKENS, D), 1.0, 6.0, ((0, 16),)),
        "expert_ids": draw_expert_ids(jax.random.fold_in(jax.random.fold_in(arg_keys[7], part), 71), part),
        "gate_weights": jnp.clip(jnp.exp(math.log(1.0) - 2.306499 * jax.random.uniform(part_splits[2], (TOKENS, TOP), jnp.float32) ** steps_of(part_splits[2], (TOKENS, TOP), ((0, 16),), -0.2, 0.2)), 0.099609375, 1.0).astype(jnp.bfloat16),
        "slots": draw_slots(jax.random.fold_in(jax.random.fold_in(arg_keys[7], part), 71), part),
        "w_gate": noise(part_splits[4], (EXPERTS, D, FF), D ** -0.5, 0.0625, ((0, 4), (2, 4))),
        "w_up": noise(part_splits[5], (EXPERTS, D, FF), D ** -0.5, 0.0625, ((0, 4), (2, 4))),
        "w_down": noise(part_splits[6], (EXPERTS, FF, D), FF ** -0.5, 0.125, ((0, 4), (1, 4))),
    }


def reference(tokens, expert_ids, gate_weights, slots, w_gate, w_up, w_down):
    experts_all = EXP_NODE * N_NODE
    matches = (expert_ids[:, :, None] == jnp.arange(experts_all, dtype=jnp.int32)[None, None, :]).astype(jnp.float32)
    token_gates = jnp.sum(gate_weights.astype(jnp.float32)[:, :, None] * matches, axis=1)
    reached = (slots < TOK_DEV).astype(jnp.float32)
    token_gates = token_gates * jnp.repeat(reached, EXP_NODE, axis=1)
    unit_share = FF // N_LOCAL

    def node_term(group):
        summed = jnp.zeros((N_LOCAL, TOKENS, D), jnp.float32)
        for member in range(EXP_NODE):
            expert = (group * EXP_NODE + member).astype(jnp.int32)
            gate_matrix = lax.dynamic_index_in_dim(w_gate, expert, 0, keepdims=False)
            up_matrix = lax.dynamic_index_in_dim(w_up, expert, 0, keepdims=False)
            down_matrix = lax.dynamic_index_in_dim(w_down, expert, 0, keepdims=False)
            gate_value = jnp.dot(tokens, gate_matrix, preferred_element_type=jnp.float32)
            up_value = jnp.dot(tokens, up_matrix, preferred_element_type=jnp.float32)
            hidden = (jax.nn.silu(gate_value) * up_value).astype(jnp.bfloat16)
            hidden_blocks = hidden.reshape(TOKENS, N_LOCAL, unit_share).astype(jnp.float32)
            down_blocks = down_matrix.reshape(N_LOCAL, unit_share, D).astype(jnp.float32)
            shares = jnp.einsum("tlf,lfd->ltd", hidden_blocks, down_blocks, precision=lax.Precision.HIGHEST)
            weight_column = lax.dynamic_index_in_dim(token_gates, expert, 1, keepdims=False)
            summed = summed + weight_column[None, :, None] * shares
        rounded = lax.optimization_barrier(summed.astype(jnp.bfloat16)).astype(jnp.float32)
        return jnp.sum(rounded, axis=0).astype(jnp.bfloat16)

    node_rows = lax.map(node_term, jnp.arange(N_NODE, dtype=jnp.int32))
    return jnp.sum(node_rows.astype(jnp.float32), axis=0).astype(jnp.bfloat16)
```

```python
import functools

import jax
import jax.numpy as jnp
from jax import lax
from jax.experimental import pallas as pl
from jax.experimental.pallas import tpu as pltpu
from jax.sharding import PartitionSpec as P

MESH = pl.DeviceIdType.MESH
LANES = 128


def split_count(width):
    for count in (7, 8, 4, 2):
        if width % (count * LANES) == 0:
            return count
    return 1


def loop(count, body):
    if count == 1:
        body(0)
    else:
        lax.fori_loop(0, count, lambda i, c: (body(i), c)[1], 0)


def kernel(N, Q, T, K, KR,
           tokens, ids, gw, slots, wg, wu, wd, out,
           X, PO, RC, RY, S2, RZ, WG, WU, WD, acc, hid, ids_v, gw_v, sl_v,
           sm, sw, sd, az_s, az_r, ay_s, ay_r, ac_s, ac_r,
           rc_s, rc_r, ry_s, ry_r, rz_s, rz_r):
    D = tokens.shape[1]
    E, _, F = wg.shape
    n = lax.axis_index("node")
    l = lax.axis_index("local")
    q, c = l // 2, lax.rem(l, 2)
    kc, nc = D // K, D // KR
    blocks = 2 * Q * N
    rows = 128 if (blocks * T) % 128 == 0 else blocks * T
    rblk = rows // T
    rcount = blocks // rblk

    def col(k):
        return pl.ds(k * kc, kc + (LANES if k == K - 1 else 0))

    def ocol(k):
        return pl.ds(k * nc, nc)

    def blk(cc, qq, nn):
        return (cc * Q + qq) * N + nn

    def to_node(d):
        return {"node": lax.rem(n + d, N)}

    def to_y(d):
        return {"local": lax.rem(q + d, Q) * 2 + c}

    to_core = {"local": q * 2 + 1 - c}

    def remote(src, dst, ss, rs, dev):
        return pltpu.make_async_remote_copy(
            src_ref=src, dst_ref=dst, send_sem=ss, recv_sem=rs,
            device_id=dev, device_id_type=MESH)

    me = blk(c, q, n)
    small = [
        pltpu.make_async_copy(tokens, X.at[me, :, pl.ds(0, D)], sm.at[0]),
        pltpu.make_async_copy(ids, ids_v, sm.at[1]),
        pltpu.make_async_copy(gw, gw_v, sm.at[2]),
        pltpu.make_async_copy(slots, sl_v, sm.at[3]),
    ]
    for cp in small:
        cp.start()
    wcp = []
    for k in range(K):
        rs = pl.ds(k * kc, kc)
        pair = [pltpu.make_async_copy(wg.at[:, rs, :], WG.at[:, rs, :], sw.at[k, 0]),
                pltpu.make_async_copy(wu.at[:, rs, :], WU.at[:, rs, :], sw.at[k, 1])]
        wcp.append(pair)
        for cp in pair:
            cp.start()
    dcp = []
    for k in range(KR):
        cp = pltpu.make_async_copy(wd.at[:, :, ocol(k)], WD.at[:, :, ocol(k)], sd.at[k])
        cp.start()
        dcp.append(cp)

    barrier = pltpu.get_barrier_semaphore()
    for d in range(1, N):
        pl.semaphore_signal(barrier, inc=1, device_id=to_node(d), device_id_type=MESH)
    for d in range(1, Q):
        pl.semaphore_signal(barrier, inc=1, device_id=to_y(d), device_id_type=MESH)
    pl.semaphore_signal(barrier, inc=1, device_id=to_core, device_id_type=MESH)

    for cp in small:
        cp.wait()
    lane = lax.broadcasted_iota(jnp.int32, (T, LANES), 1)
    gates = jnp.zeros((T, LANES), jnp.float32)
    idv, gwv, slv = ids_v[...], gw_v[...].astype(jnp.float32), sl_v[...]
    for t in range(idv.shape[1]):
        gates = gates + jnp.where(idv[:, t:t + 1] == lane, gwv[:, t:t + 1], 0.0)
    reached = jnp.zeros((T, LANES), jnp.float32)
    for g in range(N):
        mine = (lane >= g * E) & (lane < (g + 1) * E)
        reached = reached + jnp.where(mine & (slv[:, g:g + 1] < T), 1.0, 0.0)
    X[me, :, pl.ds(D, LANES)] = (gates * reached).astype(X.dtype)
    pl.semaphore_wait(barrier, N - 1 + Q - 1 + 1)

    pending = []

    def send(src, dst, ss, rs, dev):
        cp = remote(src, dst, ss, rs, dev)
        cp.start()
        pending.append(cp)

    def z_copy(k, d):
        b = X.at[me, :, col(k)]
        return b, b, az_s.at[k, d - 1], az_r.at[k, d - 1], to_node(d)

    def y_copy(k, dq, d):
        b = X.at[blk(c, q, lax.rem(n - d + N, N)), :, col(k)]
        return b, b, ay_s.at[k, dq - 1, d], ay_r.at[k, dq - 1, d], to_y(dq)

    def c_copy(k, dq):
        b = X.at[pl.ds(blk(c, lax.rem(q - dq + Q, Q), 0), N), :, col(k)]
        return b, b, ac_s.at[k, dq], ac_r.at[k, dq], to_core

    for k in range(K):
        for d in range(1, N):
            send(*z_copy(k, d))
        for dq in range(1, Q):
            send(*y_copy(k, dq, 0))

    def z_forward(k):
        for d in range(1, N):
            remote(*z_copy(k, d)).wait_recv()
            for dq in range(1, Q):
                send(*y_copy(k, dq, d))
        send(*c_copy(k, 0))

    def y_forward(k):
        for dq in range(1, Q):
            for d in range(N):
                remote(*y_copy(k, dq, d)).wait_recv()
            send(*c_copy(k, dq))

    def project(k):
        for dq in range(Q):
            remote(*c_copy(k, dq)).wait_recv()
        for cp in wcp[k]:
            cp.wait()

        def row_body(r):
            rb = pl.ds(r * rblk, rblk)
            ro = pl.ds(r * rows, rows)
            x = X[rb, :, pl.ds(k * kc, kc)].astype(jnp.float32)
            x = x.reshape(rows, kc).astype(jnp.bfloat16)

            def member(e):
                for i, W in enumerate((WG, WU)):
                    part = jnp.dot(x, W[e, pl.ds(k * kc, kc), :],
                                   preferred_element_type=jnp.float32)
                    if k == 0:
                        acc[i, e, ro, :] = part
                    else:
                        acc[i, e, ro, :] = acc[i, e, ro, :] + part

            loop(E, member)

        loop(rcount, row_body)

    for s in range(K + 2):
        if s < K:
            z_forward(s)
        if 1 <= s <= K:
            y_forward(s - 1)
        if s >= 2:
            project(s - 2)

    def hidden_body(r):
        rb = pl.ds(r * rblk, rblk)
        ro = pl.ds(r * rows, rows)
        g = X[rb, :, pl.ds(D, LANES)].astype(jnp.float32).reshape(rows, LANES)
        lanes = lax.broadcasted_iota(jnp.int32, (rows, LANES), 1)
        for e in range(E):
            w = jnp.sum(jnp.where(lanes == n * E + e, g, 0.0), axis=1, keepdims=True)
            v, u = acc[0, e, ro, :], acc[1, e, ro, :]
            h = v / (1.0 + jnp.exp(-v)) * u * w
            hid[ro, pl.ds(e * F, F)] = h.astype(hid.dtype)

    loop(rcount, hidden_body)

    half = Q * N
    step = 512 if nc % 512 == 0 else nc

    def rc_copy(k):
        return (PO.at[pl.ds((1 - c) * half, half), :, ocol(k)], RC.at[:, :, ocol(k)],
                rc_s.at[k], rc_r.at[k], to_core)

    def ry_copy(k, dq):
        return (PO.at[pl.ds(blk(c, lax.rem(q + dq, Q), 0), N), :, ocol(k)],
                RY.at[dq - 1, :, :, ocol(k)], ry_s.at[k, dq - 1], ry_r.at[k, dq - 1], to_y(dq))

    def rz_copy(k, d):
        return (S2.at[lax.rem(n + d, N), :, ocol(k)], RZ.at[d - 1, :, ocol(k)],
                rz_s.at[k, d - 1], rz_r.at[k, d - 1], to_node(d))

    def down(k):
        dcp[k].wait()

        def row_body(r):
            rb = pl.ds(r * rblk, rblk)
            h = hid[pl.ds(r * rows, rows), :]

            def col_body(j):
                cs = pl.ds(pl.multiple_of(k * nc + j * step, LANES), step)
                w = WD[:, :, cs].reshape(E * F, step)
                o = jnp.dot(h, w, preferred_element_type=jnp.float32)
                PO[rb, :, cs] = o.reshape(rblk, T, step).astype(PO.dtype)

            loop(nc // step, col_body)

        loop(rcount, row_body)
        send(*rc_copy(k))

    def core_sum(k):
        remote(*rc_copy(k)).wait_recv()
        mine = pl.ds(c * half, half)
        PO[mine, :, ocol(k)] = (PO[mine, :, ocol(k)].astype(jnp.float32)
                                + RC[:, :, ocol(k)].astype(jnp.float32)).astype(PO.dtype)
        for dq in range(1, Q):
            send(*ry_copy(k, dq))

    def y_sum(k):
        total = PO[pl.ds(blk(c, q, 0), N), :, ocol(k)].astype(jnp.float32)
        for dq in range(1, Q):
            remote(*ry_copy(k, dq)).wait_recv()
            total = total + RY[dq - 1, :, :, ocol(k)].astype(jnp.float32)
        S2[:, :, ocol(k)] = total.astype(S2.dtype)
        for d in range(1, N):
            send(*rz_copy(k, d))

    def z_sum(k):
        total = S2[n, :, ocol(k)].astype(jnp.float32)
        for d in range(1, N):
            remote(*rz_copy(k, d)).wait_recv()
            total = total + RZ[d - 1, :, ocol(k)].astype(jnp.float32)
        out[:, ocol(k)] = total.astype(out.dtype)

    for s in range(KR + 3):
        if s < KR:
            down(s)
        if 1 <= s <= KR:
            core_sum(s - 1)
        if 2 <= s <= KR + 1:
            y_sum(s - 2)
        if s >= 3:
            z_sum(s - 3)

    for cp in pending:
        cp.wait_send()


def local(N, L, tokens, ids, gw, slots, wg, wu, wd):
    Q = L // 2
    T, D = tokens.shape
    E, _, F = wg.shape
    K = KR = split_count(D)
    blocks = N * L
    bf, f32 = jnp.bfloat16, jnp.float32
    dma = pltpu.SemaphoreType.DMA
    anyspec = pl.BlockSpec(memory_space=pl.ANY)
    return pl.pallas_call(
        functools.partial(kernel, N, Q, T, K, KR),
        out_shape=jax.ShapeDtypeStruct((T, D), bf),
        in_specs=[anyspec] * 7,
        out_specs=pl.BlockSpec(memory_space=pltpu.VMEM),
        scratch_shapes=[
            pltpu.VMEM((blocks, T, D + LANES), bf),
            pltpu.VMEM((blocks, T, D), bf),
            pltpu.VMEM((Q * N, T, D), bf),
            pltpu.VMEM((Q - 1, N, T, D), bf),
            pltpu.VMEM((N, T, D), bf),
            pltpu.VMEM((N - 1, T, D), bf),
            pltpu.VMEM((E, D, F), bf),
            pltpu.VMEM((E, D, F), bf),
            pltpu.VMEM((E, F, D), bf),
            pltpu.VMEM((2, E, blocks * T, F), f32),
            pltpu.VMEM((blocks * T, E * F), bf),
            pltpu.VMEM(ids.shape, ids.dtype),
            pltpu.VMEM(gw.shape, gw.dtype),
            pltpu.VMEM(slots.shape, slots.dtype),
            dma((4,)), dma((K, 2)), dma((KR,)),
            dma((K, N - 1)), dma((K, N - 1)),
            dma((K, Q - 1, N)), dma((K, Q - 1, N)),
            dma((K, Q)), dma((K, Q)),
            dma((KR,)), dma((KR,)),
            dma((KR, Q - 1)), dma((KR, Q - 1)),
            dma((KR, N - 1)), dma((KR, N - 1)),
        ],
        compiler_params=pltpu.CompilerParams(
            collective_id=0, has_side_effects=True, vmem_limit_bytes=67043328),
    )(tokens, ids, gw, slots, wg, wu, wd)


def solution(mesh):
    N, L = mesh.shape["node"], mesh.shape["local"]
    rows = P(("parts", "node", "local"), None)
    up = P(("parts", "node"), None, "local")
    return jax.shard_map(
        functools.partial(local, N, L), mesh=mesh,
        in_specs=(rows, rows, rows, rows, up, up, P(("parts", "node"), "local", None)),
        out_specs=rows, check_vma=False)
```

```python
import functools

import jax
import jax.numpy as jnp
from jax import lax
from jax.experimental import pallas as pl
from jax.experimental.pallas import tpu as pltpu
from jax.sharding import PartitionSpec as P

MESH = pl.DeviceIdType.MESH
LANES = 128


def split_count(width):
    for count in (4, 7, 2):
        if width % (count * LANES) == 0:
            return count
    return 1


def loop(count, body):
    if count == 1:
        body(0)
    else:
        lax.fori_loop(0, count, lambda i, c: (body(i), c)[1], 0)


def kernel(N, Q, T, K, KR,
           tokens, ids, gw, slots, wg, wu, wd, out,
           X, PO, RC, RY, S2, RZ, WG, WU, WD, acc, hid, ids_v, gw_v, sl_v,
           sm, sw, sd, az_s, az_r, ay_s, ay_r, ac_s, ac_r,
           rc_s, rc_r, ry_s, ry_r, rz_s, rz_r):
    D = tokens.shape[1]
    E, _, F = wg.shape
    n = lax.axis_index("node")
    l = lax.axis_index("local")
    q, c = l // 2, lax.rem(l, 2)
    kc, nc = D // K, D // KR
    blocks = 2 * Q * N
    rows = 128 if (blocks * T) % 128 == 0 else blocks * T
    rblk = rows // T
    rcount = blocks // rblk

    def col(k):
        return pl.ds(k * kc, kc + (LANES if k == K - 1 else 0))

    def ocol(k):
        return pl.ds(k * nc, nc)

    def blk(cc, qq, nn):
        return (cc * Q + qq) * N + nn

    def to_node(d):
        return {"node": lax.rem(n + d, N)}

    def to_y(d):
        return {"local": lax.rem(q + d, Q) * 2 + c}

    to_core = {"local": q * 2 + 1 - c}

    def remote(src, dst, ss, rs, dev):
        return pltpu.make_async_remote_copy(
            src_ref=src, dst_ref=dst, send_sem=ss, recv_sem=rs,
            device_id=dev, device_id_type=MESH)

    me = blk(c, q, n)
    small = [
        pltpu.make_async_copy(tokens, X.at[me, :, pl.ds(0, D)], sm.at[0]),
        pltpu.make_async_copy(ids, ids_v, sm.at[1]),
        pltpu.make_async_copy(gw, gw_v, sm.at[2]),
        pltpu.make_async_copy(slots, sl_v, sm.at[3]),
    ]
    for cp in small:
        cp.start()
    wcp = []
    for k in range(K):
        rs = pl.ds(k * kc, kc)
        pair = [pltpu.make_async_copy(wg.at[:, rs, :], WG.at[:, rs, :], sw.at[k, 0]),
                pltpu.make_async_copy(wu.at[:, rs, :], WU.at[:, rs, :], sw.at[k, 1])]
        wcp.append(pair)
        for cp in pair:
            cp.start(priority=1)
    dcp = []
    for k in range(KR):
        cp = pltpu.make_async_copy(wd.at[:, :, ocol(k)], WD.at[:, :, ocol(k)], sd.at[k])
        cp.start(priority=1)
        dcp.append(cp)

    barrier = pltpu.get_barrier_semaphore()
    for d in range(1, N):
        pl.semaphore_signal(barrier, inc=1, device_id=to_node(d), device_id_type=MESH)
    for d in range(1, Q):
        pl.semaphore_signal(barrier, inc=1, device_id=to_y(d), device_id_type=MESH)
    pl.semaphore_signal(barrier, inc=1, device_id=to_core, device_id_type=MESH)

    for cp in small:
        cp.wait()
    lane = lax.broadcasted_iota(jnp.int32, (T, LANES), 1)
    gates = jnp.zeros((T, LANES), jnp.float32)
    idv, gwv, slv = ids_v[...], gw_v[...].astype(jnp.float32), sl_v[...].astype(jnp.float32)
    for t in range(idv.shape[1]):
        gates = gates + jnp.where(idv[:, t:t + 1] == lane, gwv[:, t:t + 1], 0.0)
    reached = jnp.zeros((T, LANES), jnp.float32)
    eye = lax.broadcasted_iota(jnp.int32, (T, T), 0) == lax.broadcasted_iota(jnp.int32, (T, T), 1)
    for g in range(N):
        slot = jnp.sum(jnp.where(eye, slv[g:g + 1, :], 0.0), axis=1, keepdims=True)
        mine = (lane >= g * E) & (lane < (g + 1) * E)
        reached = reached + jnp.where(mine & (slot < T), 1.0, 0.0)
    X[me, :, pl.ds(D, LANES)] = (gates * reached).astype(X.dtype)
    pl.semaphore_wait(barrier, N - 1 + Q - 1 + 1)

    pending = []

    def send(src, dst, ss, rs, dev):
        cp = remote(src, dst, ss, rs, dev)
        cp.start()
        pending.append(cp)

    def z_copy(k, d):
        b = X.at[me, :, col(k)]
        return b, b, az_s.at[k, d - 1], az_r.at[k, d - 1], to_node(d)

    def y_copy(k, dq, d):
        b = X.at[blk(c, q, lax.rem(n - d + N, N)), :, col(k)]
        return b, b, ay_s.at[k, dq - 1, d], ay_r.at[k, dq - 1, d], to_y(dq)

    def c_copy(k, dq):
        b = X.at[pl.ds(blk(c, lax.rem(q - dq + Q, Q), 0), N), :, col(k)]
        return b, b, ac_s.at[k, dq], ac_r.at[k, dq], to_core

    for k in range(K):
        for d in range(1, N):
            send(*z_copy(k, d))
        for dq in range(1, Q):
            send(*y_copy(k, dq, 0))

    def z_forward(k):
        for d in range(1, N):
            remote(*z_copy(k, d)).wait_recv()
            for dq in range(1, Q):
                send(*y_copy(k, dq, d))
        send(*c_copy(k, 0))

    def y_forward(k):
        for dq in range(1, Q):
            for d in range(N):
                remote(*y_copy(k, dq, d)).wait_recv()
            send(*c_copy(k, dq))

    def project(k):
        for dq in range(Q):
            remote(*c_copy(k, dq)).wait_recv()
        for cp in wcp[k]:
            cp.wait()

        def row_body(r):
            rb = pl.ds(r * rblk, rblk)
            ro = pl.ds(r * rows, rows)
            x = X[rb, :, pl.ds(k * kc, kc)].astype(jnp.float32)
            x = x.reshape(rows, kc).astype(jnp.bfloat16)

            def member(e):
                for i, W in enumerate((WG, WU)):
                    part = jnp.dot(x, W[e, pl.ds(k * kc, kc), :],
                                   preferred_element_type=jnp.float32)
                    if k == 0:
                        acc[i, e, ro, :] = part
                    else:
                        acc[i, e, ro, :] = acc[i, e, ro, :] + part

            loop(E, member)

        loop(rcount, row_body)

    for s in range(K + 2):
        if s < K:
            z_forward(s)
        if 1 <= s <= K:
            y_forward(s - 1)
        if s >= 2:
            project(s - 2)

    def hidden_body(r):
        rb = pl.ds(r * rblk, rblk)
        ro = pl.ds(r * rows, rows)
        g = X[rb, :, pl.ds(D, LANES)].astype(jnp.float32).reshape(rows, LANES)
        lanes = lax.broadcasted_iota(jnp.int32, (rows, LANES), 1)
        for e in range(E):
            w = jnp.sum(jnp.where(lanes == n * E + e, g, 0.0), axis=1, keepdims=True)
            v, u = acc[0, e, ro, :], acc[1, e, ro, :]
            h = v / (1.0 + jnp.exp(-v)) * u * w
            hid[ro, pl.ds(e * F, F)] = h.astype(hid.dtype)

    loop(rcount, hidden_body)

    half = Q * N
    step = nc // 2 if nc % (2 * LANES) == 0 else nc

    def rc_copy(k):
        return (PO.at[pl.ds((1 - c) * half, half), :, ocol(k)], RC.at[:, :, ocol(k)],
                rc_s.at[k], rc_r.at[k], to_core)

    def ry_copy(k, dq):
        return (PO.at[pl.ds(blk(c, lax.rem(q + dq, Q), 0), N), :, ocol(k)],
                RY.at[dq - 1, :, :, ocol(k)], ry_s.at[k, dq - 1], ry_r.at[k, dq - 1], to_y(dq))

    def rz_copy(k, d):
        return (S2.at[lax.rem(n + d, N), :, ocol(k)], RZ.at[d - 1, :, ocol(k)],
                rz_s.at[k, d - 1], rz_r.at[k, d - 1], to_node(d))

    def down(k):
        dcp[k].wait()

        def row_body(r):
            rb = pl.ds(r * rblk, rblk)
            h = hid[pl.ds(r * rows, rows), :]

            def col_body(j):
                cs = pl.ds(pl.multiple_of(k * nc + j * step, LANES), step)
                w = WD[:, :, cs].reshape(E * F, step)
                o = jnp.dot(h, w, preferred_element_type=jnp.float32)
                PO[rb, :, cs] = o.reshape(rblk, T, step).astype(PO.dtype)

            loop(nc // step, col_body)

        loop(rcount, row_body)
        send(*rc_copy(k))

    def core_sum(k):
        remote(*rc_copy(k)).wait_recv()
        mine = pl.ds(c * half, half)
        PO[mine, :, ocol(k)] = (PO[mine, :, ocol(k)].astype(jnp.float32)
                                + RC[:, :, ocol(k)].astype(jnp.float32)).astype(PO.dtype)
        for dq in range(1, Q):
            send(*ry_copy(k, dq))

    def y_sum(k):
        total = PO[pl.ds(blk(c, q, 0), N), :, ocol(k)].astype(jnp.float32)
        for dq in range(1, Q):
            remote(*ry_copy(k, dq)).wait_recv()
            total = total + RY[dq - 1, :, :, ocol(k)].astype(jnp.float32)
        S2[:, :, ocol(k)] = total.astype(S2.dtype)
        for d in range(1, N):
            send(*rz_copy(k, d))

    def z_sum(k):
        total = S2[n, :, ocol(k)].astype(jnp.float32)
        for d in range(1, N):
            remote(*rz_copy(k, d)).wait_recv()
            total = total + RZ[d - 1, :, ocol(k)].astype(jnp.float32)
        out[:, ocol(k)] = total.astype(out.dtype)

    for s in range(KR + 3):
        if s < KR:
            down(s)
        if 1 <= s <= KR:
            core_sum(s - 1)
        if 2 <= s <= KR + 1:
            y_sum(s - 2)
        if s >= 3:
            z_sum(s - 3)

    for cp in pending:
        cp.wait_send()


def local(N, L, tokens, ids, gw, slots, wg, wu, wd):
    Q = L // 2
    T, D = tokens.shape
    E, _, F = wg.shape
    K = KR = split_count(D)
    blocks = N * L
    bf, f32 = jnp.bfloat16, jnp.float32
    dma = pltpu.SemaphoreType.DMA
    anyspec = pl.BlockSpec(memory_space=pl.ANY)
    return pl.pallas_call(
        functools.partial(kernel, N, Q, T, K, KR),
        out_shape=jax.ShapeDtypeStruct((T, D), bf),
        in_specs=[anyspec] * 7,
        out_specs=pl.BlockSpec(memory_space=pltpu.VMEM),
        scratch_shapes=[
            pltpu.VMEM((blocks, T, D + LANES), bf),
            pltpu.VMEM((blocks, T, D), bf),
            pltpu.VMEM((Q * N, T, D), bf),
            pltpu.VMEM((Q - 1, N, T, D), bf),
            pltpu.VMEM((N, T, D), bf),
            pltpu.VMEM((N - 1, T, D), bf),
            pltpu.VMEM((E, D, F), bf),
            pltpu.VMEM((E, D, F), bf),
            pltpu.VMEM((E, F, D), bf),
            pltpu.VMEM((2, E, blocks * T, F), f32),
            pltpu.VMEM((blocks * T, E * F), bf),
            pltpu.VMEM(ids.shape, ids.dtype),
            pltpu.VMEM(gw.shape, gw.dtype),
            pltpu.VMEM(slots.shape[::-1], slots.dtype),
            dma((4,)), dma((K, 2)), dma((KR,)),
            dma((K, N - 1)), dma((K, N - 1)),
            dma((K, Q - 1, N)), dma((K, Q - 1, N)),
            dma((K, Q)), dma((K, Q)),
            dma((KR,)), dma((KR,)),
            dma((KR, Q - 1)), dma((KR, Q - 1)),
            dma((KR, N - 1)), dma((KR, N - 1)),
        ],
        compiler_params=pltpu.CompilerParams(
            collective_id=0, has_side_effects=True, vmem_limit_bytes=67043328),
    )(tokens, ids, gw, slots.T, wg, wu, wd)


def solution(mesh):
    N, L = mesh.shape["node"], mesh.shape["local"]
    rows = P(("parts", "node", "local"), None)
    up = P(("parts", "node"), None, "local")
    return jax.shard_map(
        functools.partial(local, N, L), mesh=mesh,
        in_specs=(rows, rows, rows, rows, up, up, P(("parts", "node"), "local", None)),
        out_specs=rows, check_vma=False)
```
